32 devices in a mesh: parts: 2 (over y), row: 4 (over z), col: 4 (over x, core).
Axes of the slice: x: 2, y: 2, z: 4, core: 2. Of those that a mesh axis runs over, the one named last changes fastest.
Arguments:
- state: float32 [10, 128, 512], P(None, ('parts', 'row'), 'col'), parts along dimension 1, may hold values from -5 to 5
- history: float32 [10, 128, 512], P(None, ('parts', 'row'), 'col'), parts along dimension 1, may hold values from -5 to 5
- rates: float32 [10, 10, 128, 512], P(None, None, ('parts', 'row'), 'col'), parts along dimension 2, may hold values from -2 to 2
- quadratic: float32 [10, 128, 512], P(None, ('parts', 'row'), 'col'), parts along dimension 1, may hold values from 0.1 to 1
- velocity: float32 [10, 2], replicated, may hold values from -1.5 to 1.5
- precond: float32 [10, 10, 128, 512], P(None, None, ('parts', 'row'), 'col'), parts along dimension 2, may hold values from -1 to 2, as said below
Outputs:
- updated: float32 [10, 128, 512], P(None, ('parts', 'row'), 'col'), parts along dimension 1
- lin_residual: float32 [2], P('parts'), parts along dimension 0
The draws below stay inside these ranges and needn't reach their ends.
There are 2 independent parts, one for each index of `parts`. The reference program is written for one: setup_inputs(seed, part) draws one part's arguments, and reference() takes and returns one part's arrays. A program takes and returns all parts, laid end to end along the dimension named above; an argument that names none is the same for every part. Nothing has to cross between parts.
Inputs may be any that keep to these rules, and one draw needn't show every extreme that they name: `precond`: each cell's block has diagonal entries 1 plus a spread term and independent off-diagonal entries.
All inputs are finite; a program needn't handle non-finite values.
Results may differ from the reference program's by a relative error of at most 0.00011.
Values sent between devices are 32-bit elements; how exact they have to be, the bound alone decides.
A program may use at most 64 MiB of HBM per device.

```python
import jax
import jax.numpy as jnp
from jax import lax

SPECIES = 10
KRYLOV = 4
NX = 64
NY = 512


def draw_precond(key, part):
    spread = jnp.clip(0.25 * jax.random.normal(key, (SPECIES, SPECIES, NX, NY), jnp.float32), -1.0, 1.0)
    identity = jnp.eye(SPECIES, dtype=jnp.float32)[:, :, None, None]
    return identity + spread


def block_scale(own_key, shape, pieces, least, top_value):
    def one(axis_at, shards_of):
        steps = jax.random.uniform(jax.random.fold_in(jax.random.fold_in(own_key, 6), axis_at), (shards_of,), jnp.float32, least / len(pieces), top_value / len(pieces))
        return jnp.repeat(jnp.exp(steps), shape[axis_at] // shards_of).reshape((-1,) + (1,) * (len(shape) - axis_at - 1))

    loudness = one(*pieces[0])
    for cut in pieces[1:]:
        loudness = loudness * one(*cut)
    return loudness


def centred(own_key, shape, deviation, most, cuts=(), kind=jnp.bfloat16):
    gain = block_scale(own_key, shape, cuts, -0.22, 0.18) if cuts else 1.0
    drawn = jax.random.normal(own_key, shape, jnp.float32) * deviation * gain
    return jnp.minimum(jnp.maximum(drawn, -most), most).astype(kind)


def setup_inputs(seed: int = 0, part: int = 0) -> dict:
    splits = jax.random.split(jax.random.key(seed), 7)
    own_keys = jax.random.split(jax.random.fold_in(splits[6], part), 7)
    state = centred(own_keys[0], (SPECIES, NX, NY), 1.0, 5.0, ((1, 4), (2, 4)), jnp.float32)
    history = centred(own_keys[1], (SPECIES, NX, NY), 1.0, 5.0, ((1, 4), (2, 4)), jnp.float32)
    rates = centred(own_keys[2], (SPECIES, SPECIES, NX, NY), SPECIES ** -0.5, 2.0, ((2, 4), (3, 4)), jnp.float32)
    quadratic = jnp.clip(0.1 + 0.9 * jax.random.uniform(own_keys[3], (SPECIES, NX, NY), jnp.float32) ** block_scale(own_keys[3], (SPECIES, NX, NY), ((1, 4), (2, 4)), -0.2, 0.2), 0.1, 1.0)
    velocity = jnp.clip(jax.random.uniform(splits[4], (SPECIES, 2), jnp.float32, -1.5, 1.5), -1.5, 1.5)
    precond = draw_precond(jax.random.fold_in(jax.random.fold_in(splits[6], part), 71), part)
    return dict(state=state, history=history, rates=rates, quadratic=quadratic, velocity=velocity, precond=precond)


step_gamma = 0.4
tiny_eps = 1e-12

def advect(field, velocity):
    padded = jnp.pad(field, ((0, 0), (1, 1), (1, 1)))
    along_x = padded[:, 2:, 1:-1] - padded[:, :-2, 1:-1]
    along_y = padded[:, 1:-1, 2:] - padded[:, 1:-1, :-2]
    return -0.5 * (velocity[:, 0][:, None, None] * along_x + velocity[:, 1][:, None, None] * along_y)

def blockmul(matrix, field):
    return lax.optimization_barrier(jnp.sum(matrix * field[None], axis=1))

def least_squares(hessen, beta):
    width = hessen.shape[1]
    rotated = jnp.zeros((width + 1,), jnp.float32).at[0].set(beta)
    upper = hessen
    for index in range(width):
        first = upper[index, index]
        second = upper[index + 1, index]
        radius = jnp.sqrt(first * first + second * second)
        cosine = first / radius
        sine = second / radius
        row_top = cosine * upper[index] + sine * upper[index + 1]
        row_low = -sine * upper[index] + cosine * upper[index + 1]
        upper = upper.at[index].set(row_top).at[index + 1].set(row_low)
        g_top = cosine * rotated[index] + sine * rotated[index + 1]
        g_low = -sine * rotated[index] + cosine * rotated[index + 1]
        rotated = rotated.at[index].set(g_top).at[index + 1].set(g_low)
    coef = jnp.zeros((width,), jnp.float32)
    for index in reversed(range(width)):
        partial_sum = jnp.sum(upper[index, index + 1:width] * coef[index + 1:width])
        coef = coef.at[index].set((rotated[index] - partial_sum) / upper[index, index])
    return (coef, jnp.abs(rotated[width]))

def reference(state, history, rates, quadratic, velocity, precond):
    forcing = advect(state, velocity) + blockmul(rates, state) - quadratic * state * state
    rhs = -(state - history - step_gamma * forcing)

    def apply_matrix(field):
        jac = advect(field, velocity) + blockmul(rates, field) - 2.0 * quadratic * state * field
        return field - step_gamma * jac
    beta = jnp.sqrt(jnp.sum(rhs * rhs) + tiny_eps)
    basis = [rhs / beta]
    hessen = jnp.zeros((KRYLOV + 1, KRYLOV), jnp.float32)
    for index in range(KRYLOV):
        vector = apply_matrix(blockmul(precond, basis[index]))
        stacked = jnp.stack(basis)
        dots = lax.optimization_barrier(jnp.sum(stacked * vector[None], axis=(1, 2, 3)))
        vector = vector - lax.optimization_barrier(jnp.sum(dots[:, None, None, None] * stacked, axis=0))
        size_new = jnp.sqrt(jnp.sum(vector * vector) + tiny_eps)
        hessen = hessen.at[:index + 1, index].set(dots).at[index + 1, index].set(size_new)
        basis.append(vector / size_new)
    coef, lin_norm = least_squares(hessen, beta)
    combined = lax.optimization_barrier(jnp.sum(coef[:, None, None, None] * jnp.stack(basis[:KRYLOV]), axis=0))
    updated = state + blockmul(precond, combined)
    return (updated, jnp.reshape(lin_norm, (1,)))
```

```python
import functools

import jax
import jax.numpy as jnp
from jax import lax
from jax.experimental import pallas as pl
from jax.experimental.pallas import tpu as pltpu
from jax.sharding import PartitionSpec as P

KRYLOV = 4
GAMMA = 0.4
EPS = 1e-12
SHIFT = 1.5
MESH = pl.DeviceIdType.MESH


def small_solve(gram):
    width = KRYLOV
    norm2 = gram[0][0] + EPS
    beta = jnp.sqrt(norm2)
    scale = 1.0 / norm2
    g = {(i, j): gram[j][i] * scale for j in range(width + 1) for i in range(j + 1)}
    one = jnp.ones_like(beta)
    tri = {(0, 0): one}
    inv = [one]
    sub = []
    for j in range(width + 1):
        for i in range(min(j, width)):
            value = g[i, j]
            for m in range(i):
                value = value - tri[m, i] * tri[m, j]
            tri[i, j] = value * inv[i]
        if j:
            left = g[j, j]
            for m in range(j):
                left = left - tri[m, j] * tri[m, j]
            size = jnp.sqrt(jnp.maximum(left, 0.0) * inv[j - 1] * inv[j - 1] + EPS)
            sub.append(size)
            tri[j, j] = tri[j - 1, j - 1] * size
            inv.append(1.0 / tri[j, j])
    hess = {}
    for k in range(width):
        for i in range(k + 1):
            value = tri[i, k + 1] + SHIFT * tri[i, k]
            for m in range(max(i - 1, 0), k):
                value = value - hess[i, m] * tri[m, k]
            hess[i, k] = value * inv[k]
        hess[k + 1, k] = sub[k]
    rot = [beta]
    for k in range(width):
        first, second = hess[k, k], hess[k + 1, k]
        inverse = 1.0 / jnp.sqrt(first * first + second * second)
        cosine, sine = first * inverse, second * inverse
        for j in range(k, width):
            top = hess[k, j]
            low = hess.get((k + 1, j))
            hess[k, j] = cosine * top + sine * low
            hess[k + 1, j] = cosine * low - sine * top
        rot.append(-sine * rot[k])
        rot[k] = cosine * rot[k]
    coef = [None] * width
    for k in reversed(range(width)):
        value = rot[k]
        for m in range(k + 1, width):
            value = value - hess[k, m] * coef[m]
        coef[k] = value / hess[k, k]
    out = [None] * width
    for k in reversed(range(width)):
        value = coef[k]
        for m in range(k + 1, width):
            value = value - tri[k, m] * out[m]
        out[k] = value * inv[k]
    return [c / beta for c in out], jnp.abs(rot[width])


def kernel(rows, cols, state_h, hist_h, rates_h, quad_h, vel, prec_h, out, lin,
           y, hist, rates, quad, prec, loads, vs, ds, diag, cx, cy, cs,
           put_lo, put_hi, put_t, got_lo, got_hi, got_l, got_r, ssem, rsem,
           grow, slots, gsend, grecv):
    species, high, wide = y.shape
    my_row, my_col = lax.axis_index("row"), lax.axis_index("col")
    count = rows * cols
    me = my_row * cols + my_col
    pairs = [(state_h, y), (rates_h, rates), (quad_h, quad), (hist_h, hist), (prec_h, prec)]
    copies = [pltpu.make_async_copy(a, b, loads.at[i]) for i, (a, b) in enumerate(pairs)]
    for copy in copies:
        copy.start()

    barrier = pltpu.get_barrier_semaphore()

    def other(o):
        index = lax.rem(me + o, count)
        return index, {"row": index // cols, "col": lax.rem(index, cols)}

    def greet(o, carry):
        pl.semaphore_signal(barrier, inc=1, device_id=other(o)[1], device_id_type=MESH)
        return carry

    lax.fori_loop(1, count, greet, 0)

    up, down = my_row > 0, my_row < rows - 1
    left, right = my_col > 0, my_col < cols - 1
    row_at = lax.broadcasted_iota(jnp.int32, (high, wide), 0)
    lane = lax.broadcasted_iota(jnp.int32, (high, wide), 1)
    pair = jnp.where(lane == wide - 1, 0, (lane + 1) // 2)
    edge = jnp.where(lane == 0, -1.0, jnp.where(lane == wide - 1, 1.0, 0.0))

    for there, ref in ((up, got_lo), (down, got_hi), (left, got_l), (right, got_r)):
        @pl.when(jnp.logical_not(there))
        def _(ref=ref):
            ref[...] = jnp.zeros_like(ref)

    for s in range(species):
        cx[s] = jnp.full((high, wide), 0.5 * GAMMA * vel[s, 0])
        cy[s] = jnp.full((high, wide), 0.5 * GAMMA * vel[s, 1])
        cs[s] = cy[s] * edge
    for k in range(1, KRYLOV):
        vs[k] = jnp.zeros_like(y)
    grow[...] = jnp.zeros_like(grow)

    def transfers(p):
        def make(src, dst, axis, mine, step, size, q):
            return pltpu.make_async_remote_copy(
                src_ref=src.at[p], dst_ref=dst.at[p], send_sem=ssem.at[p, q], recv_sem=rsem.at[p, q],
                device_id={axis: lax.rem(mine + step + size, size)}, device_id_type=MESH)
        return [
            (up, down, make(put_lo, got_hi, "row", my_row, -1, rows, 0)),
            (down, up, make(put_hi, got_lo, "row", my_row, 1, rows, 1)),
            (left, right, make(put_t, got_r, "col", my_col, -1, cols, 2)),
            (right, left, make(put_t, got_l, "col", my_col, 1, cols, 3)),
        ]

    def pack(p, v):
        put_lo[p] = v[:, 0:1, :]
        put_hi[p] = v[:, high - 1:high, :]
        tile = jnp.zeros((high, wide), jnp.float32)
        for s in range(species):
            moved = pltpu.roll(v[s], 2 * s, 1) if s else v[s]
            tile = jnp.where(pair == s, moved, tile)
        put_t[p] = tile

    def send(p):
        for sends, _, copy in transfers(p):
            @pl.when(sends)
            def _(copy=copy):
                copy.start()

    def receive(p):
        for _, gets, copy in transfers(p):
            @pl.when(gets)
            def _(copy=copy):
                copy.wait_recv()

    def sent(p):
        for sends, _, copy in transfers(p):
            @pl.when(sends)
            def _(copy=copy):
                copy.wait_send()

    def inner(v):
        parts = []
        for s in range(species):
            f = v[s]
            dx = jnp.where(row_at == high - 1, 0.0, pltpu.roll(f, high - 1, 0)) - jnp.where(
                row_at == 0, 0.0, pltpu.roll(f, 1, 0))
            dy = jnp.where(lane == wide - 1, 0.0, pltpu.roll(f, wide - 1, 1)) - jnp.where(
                lane == 0, 0.0, pltpu.roll(f, 1, 1))
            parts.append(cx[s] * dx + cy[s] * dy)
        return jnp.stack(parts)

    def outer(p):
        both = jnp.where(lax.rem(lane, 2) == 1, pltpu.roll(got_l[p], 2, 1), got_r[p])
        parts = []
        for s in range(species):
            moved = pltpu.roll(both, wide - 2 * s - 1, 1)
            ends = jnp.where(row_at == high - 1, got_hi[p, s], 0.0) - jnp.where(
                row_at == 0, got_lo[p, s], 0.0)
            parts.append(cx[s] * ends + cs[s] * moved)
        return jnp.stack(parts)

    def blockmul(matrix, field):
        total = matrix[:, 0] * field(0)[None]
        for t in range(1, species):
            total = total + matrix[:, t] * field(t)[None]
        return total

    def dots(k, upto):
        line = grow[...]
        at = lax.broadcasted_iota(jnp.int32, line.shape, 1)
        mine = vs[k]
        for j in range(upto):
            by_cell = jnp.sum(mine * vs[j], axis=0)
            value = jnp.sum(jnp.sum(by_cell, axis=0, keepdims=True), axis=1, keepdims=True)
            line = jnp.where(at == k * (KRYLOV + 1) + j, value, line)
        grow[...] = line

    copies[0].wait()
    pack(0, y[...])
    pl.semaphore_wait(barrier, count - 1)
    send(0)
    copies[1].wait()
    copies[2].wait()
    copies[3].wait()
    now = y[...]
    loss = quad[...] * now
    diag[...] = 1.0 + (2.0 * GAMMA) * loss
    start = hist[...] - now - GAMMA * (loss * now) + GAMMA * blockmul(rates, lambda t: y[t]) - inner(now)
    copies[4].wait()
    receive(0)
    vs[0] = start - outer(0)

    def step(k, carry):
        ds[k] = blockmul(prec, lambda t: vs[k, t])
        d = ds[k]
        pack(k + 1, d)
        send(k + 1)
        w = diag[...] * d - SHIFT * vs[k] - GAMMA * blockmul(rates, lambda t: ds[k, t]) + inner(d)
        vs[k + 1] = w
        dots(k, KRYLOV)
        receive(k + 1)
        vs[k + 1] = vs[k + 1] + outer(k + 1)
        return carry

    lax.fori_loop(0, KRYLOV, step, 0)
    dots(KRYLOV, KRYLOV + 1)
    slots[me] = grow[...]

    def share(o):
        index, where = other(o)
        put = pltpu.make_async_remote_copy(
            src_ref=grow, dst_ref=slots.at[me], send_sem=gsend.at[o], recv_sem=grecv.at[me],
            device_id=where, device_id_type=MESH)
        take = pltpu.make_async_remote_copy(
            src_ref=grow, dst_ref=slots.at[index], send_sem=gsend.at[o], recv_sem=grecv.at[index],
            device_id=where, device_id_type=MESH)
        return put, take

    def put_all(o, carry):
        share(o)[0].start()
        return carry

    def take_all(o, carry):
        share(o)[1].wait_recv()
        return carry

    def put_done(o, carry):
        share(o)[0].wait_send()
        return carry

    lax.fori_loop(1, count, put_all, 0)
    for p in range(KRYLOV + 1):
        sent(p)
    lax.fori_loop(1, count, take_all, 0)
    total = jnp.sum(slots[...], axis=0)
    at = lax.broadcasted_iota(jnp.int32, total.shape, 1)
    gram = [[jnp.sum(jnp.where(at == k * (KRYLOV + 1) + j, total, 0.0), axis=1, keepdims=True)
             for j in range(k + 1)] for k in range(KRYLOV + 1)]
    coef, residual = small_solve(gram)
    lin[0] = residual[0, 0]
    result = y[...]
    for k in range(KRYLOV):
        result = result + jnp.broadcast_to(coef[k], (high, wide))[None] * ds[k]
    out[...] = result
    lax.fori_loop(1, count, put_done, 0)


def body(rows, cols, state, history, rates, quadratic, velocity, precond):
    species, high, wide = state.shape
    field = (species, high, wide)
    phases = KRYLOV + 1
    vmem = lambda *shape: pltpu.VMEM(shape, jnp.float32)
    anywhere = pl.BlockSpec(memory_space=pl.ANY)
    updated, residual = pl.pallas_call(
        functools.partial(kernel, rows, cols),
        out_shape=(jax.ShapeDtypeStruct(field, jnp.float32), jax.ShapeDtypeStruct((1,), jnp.float32)),
        in_specs=[anywhere] * 4 + [pl.BlockSpec(memory_space=pltpu.SMEM), anywhere],
        out_specs=(pl.BlockSpec(memory_space=pltpu.VMEM), pl.BlockSpec(memory_space=pltpu.SMEM)),
        scratch_shapes=[
            vmem(*field), vmem(*field), vmem(species, *field), vmem(*field), vmem(species, *field),
            pltpu.SemaphoreType.DMA((5,)),
            vmem(phases, *field), vmem(KRYLOV, *field),
            vmem(*field), vmem(*field), vmem(*field), vmem(*field),
            vmem(phases, species, 1, wide), vmem(phases, species, 1, wide), vmem(phases, high, wide),
            vmem(phases, species, 1, wide), vmem(phases, species, 1, wide),
            vmem(phases, high, wide), vmem(phases, high, wide),
            pltpu.SemaphoreType.DMA((phases, 4)), pltpu.SemaphoreType.DMA((phases, 4)),
            vmem(1, wide), vmem(rows * cols, 1, wide),
            pltpu.SemaphoreType.DMA((rows * cols,)), pltpu.SemaphoreType.DMA((rows * cols,)),
        ],
        compiler_params=pltpu.CompilerParams(collective_id=0, has_side_effects=True),
    )(state, history, rates, quadratic, velocity, precond)
    return updated, residual


def solution(mesh):
    cells = P(None, ("parts", "row"), "col")
    blocks = P(None, None, ("parts", "row"), "col")
    return jax.shard_map(
        functools.partial(body, mesh.shape["row"], mesh.shape["col"]),
        mesh=mesh,
        in_specs=(cells, cells, blocks, cells, P(), blocks),
        out_specs=(cells, P("parts")),
        check_vma=False,
    )
```

```python
import functools

import jax
import jax.numpy as jnp
from jax import lax
from jax.experimental import pallas as pl
from jax.experimental.pallas import tpu as pltpu
from jax.sharding import PartitionSpec as P

KRYLOV = 4
GAMMA = 0.4
EPS = 1e-12
SHIFT = 1.5
MESH = pl.DeviceIdType.MESH


def small_solve(gram):
    width = KRYLOV
    norm2 = gram[0][0] + EPS
    beta = jnp.sqrt(norm2)
    scale = 1.0 / norm2
    g = {(i, j): gram[j][i] * scale for j in range(width + 1) for i in range(j + 1)}
    one = jnp.ones_like(beta)
    tri = {(0, 0): one}
    inv = [one]
    sub = []
    for j in range(width + 1):
        for i in range(min(j, width)):
            value = g[i, j]
            for m in range(i):
                value = value - tri[m, i] * tri[m, j]
            tri[i, j] = value * inv[i]
        if j:
            left = g[j, j]
            for m in range(j):
                left = left - tri[m, j] * tri[m, j]
            size = jnp.sqrt(jnp.maximum(left, 0.0) * inv[j - 1] * inv[j - 1] + EPS)
            sub.append(size)
            tri[j, j] = tri[j - 1, j - 1] * size
            inv.append(1.0 / tri[j, j])
    hess = {}
    for k in range(width):
        for i in range(k + 1):
            value = tri[i, k + 1] + SHIFT * tri[i, k]
            for m in range(max(i - 1, 0), k):
                value = value - hess[i, m] * tri[m, k]
            hess[i, k] = value * inv[k]
        hess[k + 1, k] = sub[k]
    rot = [beta]
    for k in range(width):
        first, second = hess[k, k], hess[k + 1, k]
        inverse = 1.0 / jnp.sqrt(first * first + second * second)
        cosine, sine = first * inverse, second * inverse
        for j in range(k, width):
            top = hess[k, j]
            low = hess.get((k + 1, j))
            hess[k, j] = cosine * top + sine * low
            hess[k + 1, j] = cosine * low - sine * top
        rot.append(-sine * rot[k])
        rot[k] = cosine * rot[k]
    coef = [None] * width
    for k in reversed(range(width)):
        value = rot[k]
        for m in range(k + 1, width):
            value = value - hess[k, m] * coef[m]
        coef[k] = value / hess[k, k]
    out = [None] * width
    for k in reversed(range(width)):
        value = coef[k]
        for m in range(k + 1, width):
            value = value - tri[k, m] * out[m]
        out[k] = value * inv[k]
    return [c / beta for c in out], jnp.abs(rot[width])


def kernel(rows, cols, state_h, hist_h, rates_h, quad_h, vel_h, prec_h, out, lin,
           vel, y, hist, rates, quad, prec, loads, vs, ds, diag, cx, cy, cs,
           put_lo, put_hi, put_t, got_lo, got_hi, got_l, got_r, ssem, rsem,
           grow, slots, gsend, grecv):
    species, high, wide = y.shape
    my_row, my_col = lax.axis_index("row"), lax.axis_index("col")
    count = rows * cols
    me = my_row * cols + my_col
    pairs = [(state_h, y), (vel_h, vel), (rates_h, rates), (quad_h, quad), (hist_h, hist), (prec_h, prec)]
    copies = [pltpu.make_async_copy(a, b, loads.at[i]) for i, (a, b) in enumerate(pairs)]
    for copy in copies:
        copy.start()

    barrier = pltpu.get_barrier_semaphore()

    def other(o):
        index = lax.rem(me + o, count)
        return index, {"row": index // cols, "col": lax.rem(index, cols)}

    def greet(o, carry):
        pl.semaphore_signal(barrier, inc=1, device_id=other(o)[1], device_id_type=MESH)
        return carry


    near = rows + cols - 2 <= KRYLOV + 2
    up, down = my_row > 0, my_row < rows - 1
    left, right = my_col > 0, my_col < cols - 1
    if near:
        for there, axis, at in ((up, "row", my_row - 1), (down, "row", my_row + 1), (left, "col", my_col - 1), (right, "col", my_col + 1)):
            @pl.when(there)
            def _(axis=axis, at=at):
                pl.semaphore_signal(barrier, inc=1, device_id={axis: at}, device_id_type=MESH)
    else:
        lax.fori_loop(1, count, greet, 0)

    row_at = lax.broadcasted_iota(jnp.int32, (high, wide), 0)
    lane = lax.broadcasted_iota(jnp.int32, (high, wide), 1)
    pair = jnp.where(lane == wide - 1, 0, (lane + 1) // 2)
    edge = jnp.where(lane == 0, -1.0, jnp.where(lane == wide - 1, 1.0, 0.0))

    for there, ref in ((up, got_lo), (down, got_hi), (left, got_l), (right, got_r)):
        @pl.when(jnp.logical_not(there))
        def _(ref=ref):
            ref[...] = jnp.zeros_like(ref)

    def transfers(p):
        def make(src, dst, axis, mine, step, size, q):
            return pltpu.make_async_remote_copy(
                src_ref=src.at[p], dst_ref=dst.at[p], send_sem=ssem.at[p, q], recv_sem=rsem.at[p, q],
                device_id={axis: lax.rem(mine + step + size, size)}, device_id_type=MESH)
        return [
            (up, down, make(put_lo, got_hi, "row", my_row, -1, rows, 0)),
            (down, up, make(put_hi, got_lo, "row", my_row, 1, rows, 1)),
            (left, right, make(put_t, got_r, "col", my_col, -1, cols, 2)),
            (right, left, make(put_t, got_l, "col", my_col, 1, cols, 3)),
        ]

    def pack(p, v):
        for s in range(species):
            put_lo[p, s:s + 1, :] = v[s, 0:1, :]
            put_hi[p, s:s + 1, :] = v[s, high - 1:high, :]
        tile = jnp.zeros((high, wide), jnp.float32)
        for s in range(species):
            moved = pltpu.roll(v[s], 2 * s, 1) if s else v[s]
            tile = jnp.where(pair == s, moved, tile)
        put_t[p] = tile

    def send(p):
        for sends, _, copy in transfers(p):
            @pl.when(sends)
            def _(copy=copy):
                copy.start()

    def receive(p):
        for _, gets, copy in transfers(p):
            @pl.when(gets)
            def _(copy=copy):
                copy.wait_recv()

    def sent(p):
        for sends, _, copy in transfers(p):
            @pl.when(sends)
            def _(copy=copy):
                copy.wait_send()

    def inner(v):
        parts = []
        for s in range(species):
            f = v[s]
            dx = jnp.where(row_at == high - 1, 0.0, pltpu.roll(f, high - 1, 0)) - jnp.where(
                row_at == 0, 0.0, pltpu.roll(f, 1, 0))
            dy = jnp.where(lane == wide - 1, 0.0, pltpu.roll(f, wide - 1, 1)) - jnp.where(
                lane == 0, 0.0, pltpu.roll(f, 1, 1))
            parts.append(cx[s] * dx + cy[s] * dy)
        return jnp.stack(parts)

    def outer(p):
        both = jnp.where(lax.rem(lane, 2) == 1, pltpu.roll(got_l[p], 2, 1), got_r[p])
        parts = []
        for s in range(species):
            moved = pltpu.roll(both, wide - 2 * s - 1, 1)
            ends = jnp.where(row_at == high - 1, got_hi[p, s:s + 1, :], 0.0) - jnp.where(
                row_at == 0, got_lo[p, s:s + 1, :], 0.0)
            parts.append(cx[s] * ends + cs[s] * moved)
        return jnp.stack(parts)

    def blockmul(matrix, field):
        total = matrix[:, 0] * field(0)[None]
        for t in range(1, species):
            total = total + matrix[:, t] * field(t)[None]
        return total

    def dots(k, upto):
        line = grow[...]
        at = lax.broadcasted_iota(jnp.int32, line.shape, 1)
        mine = vs[k]
        for j in range(upto):
            by_cell = jnp.sum(mine * vs[j], axis=0)
            value = jnp.sum(jnp.sum(by_cell, axis=0, keepdims=True), axis=1, keepdims=True)
            line = jnp.where(at == k * (KRYLOV + 1) + j, value, line)
        grow[...] = line

    copies[0].wait()
    pack(0, y[...])
    if near:
        beside = sum(there.astype(jnp.int32) for there in (up, down, left, right))
        pl.semaphore_wait(barrier, beside)
    else:
        pl.semaphore_wait(barrier, count - 1)
    send(0)
    copies[1].wait()
    for s in range(species):
        cx[s] = jnp.full((high, wide), 0.5 * GAMMA * vel[0, s])
        cy[s] = jnp.full((high, wide), 0.5 * GAMMA * vel[1, s])
        cs[s] = cy[s] * edge
    for k in range(1, KRYLOV):
        vs[k] = jnp.zeros_like(y)
    grow[...] = jnp.zeros_like(grow)
    for copy in copies[2:5]:
        copy.wait()
    now = y[...]
    loss = quad[...] * now
    diag[...] = 1.0 + (2.0 * GAMMA) * loss
    start = hist[...] - now - GAMMA * (loss * now) + GAMMA * blockmul(rates, lambda t: y[t]) - inner(now)
    copies[5].wait()
    receive(0)
    vs[0] = start - outer(0)

    def step(k, carry):
        ds[k] = blockmul(prec, lambda t: vs[k, t])
        d = ds[k]
        pack(k + 1, d)
        send(k + 1)
        w = diag[...] * d - SHIFT * vs[k] - GAMMA * blockmul(rates, lambda t: ds[k, t]) + inner(d)
        vs[k + 1] = w
        dots(k, KRYLOV)
        receive(k + 1)
        vs[k + 1] = vs[k + 1] + outer(k + 1)
        return carry

    lax.fori_loop(0, KRYLOV, step, 0)
    dots(KRYLOV, KRYLOV + 1)
    slots[me] = grow[...]

    def share(o):
        index, where = other(o)
        put = pltpu.make_async_remote_copy(
            src_ref=grow, dst_ref=slots.at[me], send_sem=gsend.at[o], recv_sem=grecv.at[me],
            device_id=where, device_id_type=MESH)
        take = pltpu.make_async_remote_copy(
            src_ref=grow, dst_ref=slots.at[index], send_sem=gsend.at[o], recv_sem=grecv.at[index],
            device_id=where, device_id_type=MESH)
        return put, take

    def put_all(o, carry):
        share(o)[0].start()
        return carry

    def take_all(o, carry):
        share(o)[1].wait_recv()
        return carry

    def put_done(o, carry):
        share(o)[0].wait_send()
        return carry

    lax.fori_loop(1, count, put_all, 0)
    for p in range(KRYLOV + 1):
        sent(p)
    lax.fori_loop(1, count, take_all, 0)
    total = jnp.sum(slots[...], axis=0)
    at = lax.broadcasted_iota(jnp.int32, total.shape, 1)
    gram = [[jnp.sum(jnp.where(at == k * (KRYLOV + 1) + j, total, 0.0), axis=1, keepdims=True)
             for j in range(k + 1)] for k in range(KRYLOV + 1)]
    coef, residual = small_solve(gram)
    lin[0] = residual[0, 0]
    result = y[...]
    for k in range(KRYLOV):
        result = result + jnp.broadcast_to(coef[k], (high, wide))[None] * ds[k]
    out[...] = result
    lax.fori_loop(1, count, put_done, 0)


def body(rows, cols, state, history, rates, quadratic, velocity, precond):
    species, high, wide = state.shape
    field = (species, high, wide)
    phases = KRYLOV + 1
    vmem = lambda *shape: pltpu.VMEM(shape, jnp.float32)
    anywhere = pl.BlockSpec(memory_space=pl.ANY)
    updated, residual = pl.pallas_call(
        functools.partial(kernel, rows, cols),
        out_shape=(pltpu.VMEM(field, jnp.float32), jax.ShapeDtypeStruct((1,), jnp.float32)),
        in_specs=[anywhere] * 6,
        out_specs=(pl.BlockSpec(memory_space=pltpu.VMEM), pl.BlockSpec(memory_space=pltpu.SMEM)),
        scratch_shapes=[
            pltpu.SMEM(velocity.shape[::-1], jnp.float32),
            vmem(*field), vmem(*field), vmem(species, *field), vmem(*field), vmem(species, *field),
            pltpu.SemaphoreType.DMA((6,)),
            vmem(phases, *field), vmem(KRYLOV, *field),
            vmem(*field), vmem(*field), vmem(*field), vmem(*field),
            vmem(phases, species, wide), vmem(phases, species, wide), vmem(phases, high, wide),
            vmem(phases, species, wide), vmem(phases, species, wide),
            vmem(phases, high, wide), vmem(phases, high, wide),
            pltpu.SemaphoreType.DMA((phases, 4)), pltpu.SemaphoreType.DMA((phases, 4)),
            vmem(1, wide), vmem(rows * cols, 1, wide),
            pltpu.SemaphoreType.DMA((rows * cols,)), pltpu.SemaphoreType.DMA((rows * cols,)),
        ],
        compiler_params=pltpu.CompilerParams(collective_id=0, has_side_effects=True),
    )(state, history, rates, quadratic, velocity.T, precond)
    return updated, residual


def solution(mesh):
    cells = P(None, ("parts", "row"), "col")
    blocks = P(None, None, ("parts", "row"), "col")
    return jax.shard_map(
        functools.partial(body, mesh.shape["row"], mesh.shape["col"]),
        mesh=mesh,
        in_specs=(cells, cells, blocks, cells, P(), blocks),
        out_specs=(cells, P("parts")),
        check_vma=False,
    )
```

```python
import functools

import jax
import jax.numpy as jnp
from jax import lax
from jax.experimental import pallas as pl
from jax.experimental.pallas import tpu as pltpu
from jax.sharding import PartitionSpec as P

KRYLOV = 4
GAMMA = 0.4
EPS = 1e-12
SHIFT = 1.5
MESH = pl.DeviceIdType.MESH


def small_solve(gram):
    width = KRYLOV
    norm2 = gram[0][0] + EPS
    beta = jnp.sqrt(norm2)
    scale = 1.0 / norm2
    g = {(i, j): gram[j][i] * scale for j in range(width + 1) for i in range(j + 1)}
    one = jnp.ones_like(beta)
    tri = {(0, 0): one}
    inv = [one]
    sub = []
    for j in range(width + 1):
        for i in range(min(j, width)):
            value = g[i, j]
            for m in range(i):
                value = value - tri[m, i] * tri[m, j]
            tri[i, j] = value * inv[i]
        if j:
            left = g[j, j]
            for m in range(j):
                left = left - tri[m, j] * tri[m, j]
            size = jnp.sqrt(jnp.maximum(left, 0.0) * inv[j - 1] * inv[j - 1] + EPS)
            sub.append(size)
            tri[j, j] = tri[j - 1, j - 1] * size
            inv.append(1.0 / tri[j, j])
    hess = {}
    for k in range(width):
        for i in range(k + 1):
            value = tri[i, k + 1] + SHIFT * tri[i, k]
            for m in range(max(i - 1, 0), k):
                value = value - hess[i, m] * tri[m, k]
            hess[i, k] = value * inv[k]
        hess[k + 1, k] = sub[k]
    rot = [beta]
    for k in range(width):
        first, second = hess[k, k], hess[k + 1, k]
        inverse = 1.0 / jnp.sqrt(first * first + second * second)
        cosine, sine = first * inverse, second * inverse
        for j in range(k, width):
            top = hess[k, j]
            low = hess.get((k + 1, j))
            hess[k, j] = cosine * top + sine * low
            hess[k + 1, j] = cosine * low - sine * top
        rot.append(-sine * rot[k])
        rot[k] = cosine * rot[k]
    coef = [None] * width
    for k in reversed(range(width)):
        value = rot[k]
        for m in range(k + 1, width):
            value = value - hess[k, m] * coef[m]
        coef[k] = value / hess[k, k]
    out = [None] * width
    for k in reversed(range(width)):
        value = coef[k]
        for m in range(k + 1, width):
            value = value - tri[k, m] * out[m]
        out[k] = value * inv[k]
    return [c / beta for c in out], jnp.abs(rot[width])


def kernel(rows, cols, state_h, hist_h, rates_h, quad_h, vel_h, prec_h, out, lin,
           vel, y, hist, rates, quad, prec, loads, vs, ds, diag, cx, cy, cs,
           put_lo, put_hi, put_t, got_lo, got_hi, got_l, got_r, ssem, rsem,
           grow, slots, gsend, grecv,
           pput_lo, pput_hi, pput_t, pgot_lo, pgot_hi, pgot_l, pgot_r, psend, precv, got_c, csend, crecv):
    species, high, wide = y.shape
    my_row, my_col = lax.axis_index("row"), lax.axis_index("col")
    count = rows * cols
    me = my_row * cols + my_col
    pairs = [(state_h, y), (vel_h, vel), (rates_h, rates), (quad_h, quad), (hist_h, hist), (prec_h, prec)]
    copies = [pltpu.make_async_copy(a, b, loads.at[i]) for i, (a, b) in enumerate(pairs)]
    for copy in copies:
        copy.start()

    barrier = pltpu.get_barrier_semaphore()

    def other(o):
        index = lax.rem(me + o, count)
        return index, {"row": index // cols, "col": lax.rem(index, cols)}

    def greet(o, carry):
        pl.semaphore_signal(barrier, inc=1, device_id=other(o)[1], device_id_type=MESH)
        return carry


    near = rows <= 4 and cols <= 4
    up, down = my_row > 0, my_row < rows - 1
    left, right = my_col > 0, my_col < cols - 1
    if near:
        for there, axis, at in ((up, "row", my_row - 1), (down, "row", my_row + 1), (left, "col", my_col - 1), (right, "col", my_col + 1)):
            @pl.when(there)
            def _(axis=axis, at=at):
                pl.semaphore_signal(barrier, inc=1, device_id={axis: at}, device_id_type=MESH)
    else:
        lax.fori_loop(1, count, greet, 0)

    row_at = lax.broadcasted_iota(jnp.int32, (high, wide), 0)
    lane = lax.broadcasted_iota(jnp.int32, (high, wide), 1)
    pair = jnp.where(lane == wide - 1, 0, (lane + 1) // 2)
    edge = jnp.where(lane == 0, -1.0, jnp.where(lane == wide - 1, 1.0, 0.0))

    for there, ref in ((up, got_lo), (down, got_hi), (left, got_l), (right, got_r), (up, pgot_lo), (down, pgot_hi),
                       (left, pgot_l), (right, pgot_r)):
        @pl.when(jnp.logical_not(there))
        def _(ref=ref):
            ref[...] = jnp.zeros_like(ref)

    corners = []
    for q, (dr, dc) in enumerate(((1, 1), (1, -1), (-1, 1), (-1, -1))):
        sends = jnp.logical_and(down if dr > 0 else up, right if dc > 0 else left)
        gets = jnp.logical_and(up if dr > 0 else down, left if dc > 0 else right)
        corners.append((q, dr, dc, sends, gets))

        @pl.when(jnp.logical_not(gets))
        def _(q=q):
            for p in range(1, KRYLOV, 2):
                got_c[p, q] = jnp.zeros((1, wide), jnp.float32)

    def diagonals(p):
        made = []
        for q, dr, dc, sends, gets in corners:
            at = high - 1 if dr > 0 else 0
            made.append((sends, gets, pltpu.make_async_remote_copy(
                src_ref=put_t.at[p, at:at + 1], dst_ref=got_c.at[p, q],
                send_sem=csend.at[p, q], recv_sem=crecv.at[p, q],
                device_id={"row": lax.rem(my_row + dr + rows, rows), "col": lax.rem(my_col + dc + cols, cols)},
                device_id_type=MESH)))
        return made

    def blocks():
        def make(src, dst, axis, mine, step, size, q):
            return pltpu.make_async_remote_copy(
                src_ref=src, dst_ref=dst, send_sem=psend.at[q], recv_sem=precv.at[q],
                device_id={axis: lax.rem(mine + step + size, size)}, device_id_type=MESH)
        return [
            (up, down, make(pput_lo, pgot_hi, "row", my_row, -1, rows, 0)),
            (down, up, make(pput_hi, pgot_lo, "row", my_row, 1, rows, 1)),
            (left, right, make(pput_t, pgot_r, "col", my_col, -1, cols, 2)),
            (right, left, make(pput_t, pgot_l, "col", my_col, 1, cols, 3)),
        ]

    def transfers(p):
        def make(src, dst, axis, mine, step, size, q):
            return pltpu.make_async_remote_copy(
                src_ref=src.at[p], dst_ref=dst.at[p], send_sem=ssem.at[p, q], recv_sem=rsem.at[p, q],
                device_id={axis: lax.rem(mine + step + size, size)}, device_id_type=MESH)
        return [
            (up, down, make(put_lo, got_hi, "row", my_row, -1, rows, 0)),
            (down, up, make(put_hi, got_lo, "row", my_row, 1, rows, 1)),
            (left, right, make(put_t, got_r, "col", my_col, -1, cols, 2)),
            (right, left, make(put_t, got_l, "col", my_col, 1, cols, 3)),
        ]

    def tile_of(v):
        tile = jnp.zeros((high, wide), jnp.float32)
        for s in range(species):
            moved = pltpu.roll(v[s], 2 * s, 1) if s else v[s]
            tile = jnp.where(pair == s, moved, tile)
        return tile

    def pack(p, v):
        for s in range(species):
            put_lo[p, s:s + 1, :] = v[s, 0:1, :]
            put_hi[p, s:s + 1, :] = v[s, high - 1:high, :]
        put_t[p] = tile_of(v)

    def pack_blocks():
        def one(t, carry):
            block = prec[:, t]
            for s in range(species):
                pput_lo[t, s:s + 1, :] = block[s, 0:1, :]
                pput_hi[t, s:s + 1, :] = block[s, high - 1:high, :]
            pput_t[t] = tile_of(block)
            return carry
        lax.fori_loop(0, species, one, 0)

    def send(made):
        for sends, _, copy in made:
            @pl.when(sends)
            def _(copy=copy):
                copy.start()

    def receive(made):
        for _, gets, copy in made:
            @pl.when(gets)
            def _(copy=copy):
                copy.wait_recv()

    def sent(made):
        for sends, _, copy in made:
            @pl.when(sends)
            def _(copy=copy):
                copy.wait_send()

    def complete(k, p):
        low, top = got_lo[p + 1], got_hi[p + 1]
        west, east = got_l[p + 1], got_r[p + 1]
        first = lax.broadcasted_iota(jnp.int32, (1, wide), 1) == 0
        near_row, far_row = row_at == 0, row_at == high - 1
        lines = [got_c[p, q] for q in range(4)]
        for t in range(species):
            d = ds[k, t]
            odd, even = (2 * t - 1) % wide, 2 * t
            ul, dl = lines[0][:, odd:odd + 1], lines[2][:, odd:odd + 1]
            ur, dr = lines[1][:, even:even + 1], lines[3][:, even:even + 1]
            ax, ay, ends = cx[t], cy[t], cs[t, 0:1, :]
            low = low + pgot_lo[t] * (ax[0:1] * d[0:1] + ends * jnp.where(first, ul, ur))
            top = top + pgot_hi[t] * (ends * jnp.where(first, dl, dr) - ax[0:1] * d[high - 1:high])
            side_l = jnp.where(near_row, -ul, jnp.where(far_row, dl, 0.0))
            side_r = jnp.where(near_row, -ur, jnp.where(far_row, dr, 0.0))
            west = west + pgot_l[t] * (ax * side_l + ay * d[:, 0:1])
            east = east + pgot_r[t] * (ax * side_r - ay * d[:, wide - 1:wide])
        got_lo[p + 1] = low
        got_hi[p + 1] = top
        got_l[p + 1] = west
        got_r[p + 1] = east

    def inner(v):
        parts = []
        for s in range(species):
            f = v[s]
            dx = jnp.where(row_at == high - 1, 0.0, pltpu.roll(f, high - 1, 0)) - jnp.where(
                row_at == 0, 0.0, pltpu.roll(f, 1, 0))
            dy = jnp.where(lane == wide - 1, 0.0, pltpu.roll(f, wide - 1, 1)) - jnp.where(
                lane == 0, 0.0, pltpu.roll(f, 1, 1))
            parts.append(cx[s] * dx + cy[s] * dy)
        return jnp.stack(parts)

    def outer(p):
        both = jnp.where(lax.rem(lane, 2) == 1, pltpu.roll(got_l[p], 2, 1), got_r[p])
        parts = []
        for s in range(species):
            moved = pltpu.roll(both, wide - 2 * s - 1, 1)
            ends = jnp.where(row_at == high - 1, got_hi[p, s:s + 1, :], 0.0) - jnp.where(
                row_at == 0, got_lo[p, s:s + 1, :], 0.0)
            parts.append(cx[s] * ends + cs[s] * moved)
        return jnp.stack(parts)

    def blockmul(matrix, field):
        total = matrix[:, 0] * field(0)[None]
        for t in range(1, species):
            total = total + matrix[:, t] * field(t)[None]
        return total

    def dots(k, upto):
        line = grow[...]
        at = lax.broadcasted_iota(jnp.int32, line.shape, 1)
        mine = vs[k]
        for j in range(upto):
            by_cell = jnp.sum(mine * vs[j], axis=0)
            value = jnp.sum(jnp.sum(by_cell, axis=0, keepdims=True), axis=1, keepdims=True)
            line = jnp.where(at == k * (KRYLOV + 1) + j, value, line)
        grow[...] = line

    copies[0].wait()
    pack(0, y[...])
    if near:
        beside = sum(there.astype(jnp.int32) for there in (up, down, left, right))
        pl.semaphore_wait(barrier, beside)
    else:
        pl.semaphore_wait(barrier, count - 1)
    send(transfers(0))
    copies[1].wait()
    for s in range(species):
        cx[s] = jnp.full((high, wide), 0.5 * GAMMA * vel[0, s])
        cy[s] = jnp.full((high, wide), 0.5 * GAMMA * vel[1, s])
        cs[s] = cy[s] * edge
    for k in range(1, KRYLOV):
        vs[k] = jnp.zeros_like(y)
    grow[...] = jnp.zeros_like(grow)
    for copy in copies[2:5]:
        copy.wait()
    now = y[...]
    copies[5].wait()
    pack_blocks()
    send(blocks())
    loss = quad[...] * now
    diag[...] = 1.0 + (2.0 * GAMMA) * loss
    start = hist[...] - now - GAMMA * (loss * now) + GAMMA * blockmul(rates, lambda t: y[t]) - inner(now)
    receive(transfers(0))
    vs[0] = start - outer(0)

    def apply(k):
        return diag[...] * ds[k] - SHIFT * vs[k] - GAMMA * blockmul(rates, lambda t: ds[k, t]) + inner(ds[k])

    def two_steps(j, carry):
        k, p = 2 * j, 2 * j + 1
        ds[k] = blockmul(prec, lambda t: vs[k, t])
        pack(p, ds[k])
        send(transfers(p))
        send(diagonals(p))
        vs[k + 1] = apply(k)
        pack(p + 1, blockmul(prec, lambda t: vs[k + 1, t]))
        send(transfers(p + 1))
        dots(k, KRYLOV)

        @pl.when(j == 0)
        def _():
            receive(blocks())

        receive(transfers(p))
        vs[k + 1] = vs[k + 1] + outer(p)
        ds[k + 1] = blockmul(prec, lambda t: vs[k + 1, t])
        vs[k + 2] = apply(k + 1)
        dots(k + 1, KRYLOV)
        receive(transfers(p + 1))
        receive(diagonals(p))
        complete(k, p)
        vs[k + 2] = vs[k + 2] + outer(p + 1)
        return carry

    lax.fori_loop(0, KRYLOV // 2, two_steps, 0)
    dots(KRYLOV, KRYLOV + 1)
    slots[me] = grow[...]

    def share(o):
        index, where = other(o)
        put = pltpu.make_async_remote_copy(
            src_ref=grow, dst_ref=slots.at[me], send_sem=gsend.at[o], recv_sem=grecv.at[me],
            device_id=where, device_id_type=MESH)
        take = pltpu.make_async_remote_copy(
            src_ref=grow, dst_ref=slots.at[index], send_sem=gsend.at[o], recv_sem=grecv.at[index],
            device_id=where, device_id_type=MESH)
        return put, take

    def put_all(o, carry):
        share(o)[0].start()
        return carry

    def take_all(o, carry):
        share(o)[1].wait_recv()
        return carry

    def put_done(o, carry):
        share(o)[0].wait_send()
        return carry

    lax.fori_loop(1, count, put_all, 0)
    for p in range(KRYLOV + 1):
        sent(transfers(p))
    for p in range(1, KRYLOV, 2):
        sent(diagonals(p))
    sent(blocks())
    lax.fori_loop(1, count, take_all, 0)
    total = jnp.sum(slots[...], axis=0)
    at = lax.broadcasted_iota(jnp.int32, total.shape, 1)
    gram = [[jnp.sum(jnp.where(at == k * (KRYLOV + 1) + j, total, 0.0), axis=1, keepdims=True)
             for j in range(k + 1)] for k in range(KRYLOV + 1)]
    coef, residual = small_solve(gram)
    lin[0] = residual[0, 0]
    result = y[...]
    for k in range(KRYLOV):
        result = result + jnp.broadcast_to(coef[k], (high, wide))[None] * ds[k]
    out[...] = result
    lax.fori_loop(1, count, put_done, 0)


def body(rows, cols, state, history, rates, quadratic, velocity, precond):
    species, high, wide = state.shape
    field = (species, high, wide)
    phases = KRYLOV + 1
    vmem = lambda *shape: pltpu.VMEM(shape, jnp.float32)
    anywhere = pl.BlockSpec(memory_space=pl.ANY)
    updated, residual = pl.pallas_call(
        functools.partial(kernel, rows, cols),
        out_shape=(pltpu.VMEM(field, jnp.float32), jax.ShapeDtypeStruct((1,), jnp.float32)),
        in_specs=[anywhere] * 6,
        out_specs=(pl.BlockSpec(memory_space=pltpu.VMEM), pl.BlockSpec(memory_space=pltpu.SMEM)),
        scratch_shapes=[
            pltpu.SMEM(velocity.shape[::-1], jnp.float32),
            vmem(*field), vmem(*field), vmem(species, *field), vmem(*field), vmem(species, *field),
            pltpu.SemaphoreType.DMA((6,)),
            vmem(phases, *field), vmem(KRYLOV, *field),
            vmem(*field), vmem(*field), vmem(*field), vmem(*field),
            vmem(phases, species, wide), vmem(phases, species, wide), vmem(phases, high, wide),
            vmem(phases, species, wide), vmem(phases, species, wide),
            vmem(phases, high, wide), vmem(phases, high, wide),
            pltpu.SemaphoreType.DMA((phases, 4)), pltpu.SemaphoreType.DMA((phases, 4)),
            vmem(1, wide), vmem(rows * cols, 1, wide),
            pltpu.SemaphoreType.DMA((rows * cols,)), pltpu.SemaphoreType.DMA((rows * cols,)),
            vmem(species, species, wide), vmem(species, species, wide), vmem(species, high, wide),
            vmem(species, species, wide), vmem(species, species, wide),
            vmem(species, high, wide), vmem(species, high, wide),
            pltpu.SemaphoreType.DMA((4,)), pltpu.SemaphoreType.DMA((4,)),
            vmem(phases, 4, 1, wide),
            pltpu.SemaphoreType.DMA((phases, 4)), pltpu.SemaphoreType.DMA((phases, 4)),
        ],
        compiler_params=pltpu.CompilerParams(collective_id=0, has_side_effects=True),
    )(state, history, rates, quadratic, velocity.T, precond)
    return updated, residual


def solution(mesh):
    cells = P(None, ("parts", "row"), "col")
    blocks = P(None, None, ("parts", "row"), "col")
    return jax.shard_map(
        functools.partial(body, mesh.shape["row"], mesh.shape["col"]),
        mesh=mesh,
        in_specs=(cells, cells, blocks, cells, P(), blocks),
        out_specs=(cells, P("parts")),
        check_vma=False,
    )
```

```python
import functools

import jax
import jax.numpy as jnp
from jax import lax
from jax.experimental import pallas as pl
from jax.experimental.pallas import tpu as pltpu
from jax.sharding import PartitionSpec as P

KRYLOV = 4
GAMMA = 0.4
EPS = 1e-12
SHIFT = 1.5
MESH = pl.DeviceIdType.MESH


def small_solve(gram):
    width = KRYLOV
    norm2 = gram[0][0] + EPS
    beta = jnp.sqrt(norm2)
    scale = 1.0 / norm2
    g = {(i, j): gram[j][i] * scale for j in range(width + 1) for i in range(j + 1)}
    one = jnp.ones_like(beta)
    tri = {(0, 0): one}
    inv = [one]
    sub = []
    for j in range(width + 1):
        for i in range(min(j, width)):
            value = g[i, j]
            for m in range(i):
                value = value - tri[m, i] * tri[m, j]
            tri[i, j] = value * inv[i]
        if j:
            left = g[j, j]
            for m in range(j):
                left = left - tri[m, j] * tri[m, j]
            size = jnp.sqrt(jnp.maximum(left, 0.0) * inv[j - 1] * inv[j - 1] + EPS)
            sub.append(size)
            tri[j, j] = tri[j - 1, j - 1] * size
            inv.append(1.0 / tri[j, j])
    hess = {}
    for k in range(width):
        for i in range(k + 1):
            value = tri[i, k + 1] + SHIFT * tri[i, k]
            for m in range(max(i - 1, 0), k):
                value = value - hess[i, m] * tri[m, k]
            hess[i, k] = value * inv[k]
        hess[k + 1, k] = sub[k]
    rot = [beta]
    for k in range(width):
        first, second = hess[k, k], hess[k + 1, k]
        inverse = 1.0 / jnp.sqrt(first * first + second * second)
        cosine, sine = first * inverse, second * inverse
        for j in range(k, width):
            top = hess[k, j]
            low = hess.get((k + 1, j))
            hess[k, j] = cosine * top + sine * low
            hess[k + 1, j] = cosine * low - sine * top
        rot.append(-sine * rot[k])
        rot[k] = cosine * rot[k]
    coef = [None] * width
    for k in reversed(range(width)):
        value = rot[k]
        for m in range(k + 1, width):
            value = value - hess[k, m] * coef[m]
        coef[k] = value / hess[k, k]
    out = [None] * width
    for k in reversed(range(width)):
        value = coef[k]
        for m in range(k + 1, width):
            value = value - tri[k, m] * out[m]
        out[k] = value * inv[k]
    return [c / beta for c in out], jnp.abs(rot[width])


def kernel(rows, cols, state_h, hist_h, rates_h, quad_h, vel_h, prec_h, out, lin,
           vel, y, hist, rates, quad, prec, loads, vs, ds, diag, cx, cy, cs,
           put_lo, put_hi, put_t, got_lo, got_hi, got_l, got_r, ssem, rsem,
           grow, slots, gsend, grecv,
           pput_lo, pput_hi, pput_t, pgot_lo, pgot_hi, pgot_l, pgot_r, psend, precv, got_c, csend, crecv):
    species, high, wide = y.shape
    my_row, my_col = lax.axis_index("row"), lax.axis_index("col")
    count = rows * cols
    me = my_row * cols + my_col
    pairs = [(state_h, y), (vel_h, vel), (rates_h, rates), (quad_h, quad), (hist_h, hist), (prec_h, prec)]
    copies = [pltpu.make_async_copy(a, b, loads.at[i]) for i, (a, b) in enumerate(pairs)]
    for copy in copies:
        copy.start()

    barrier = pltpu.get_barrier_semaphore()

    def other(o):
        index = lax.rem(me + o, count)
        return index, {"row": index // cols, "col": lax.rem(index, cols)}

    def greet(o, carry):
        pl.semaphore_signal(barrier, inc=1, device_id=other(o)[1], device_id_type=MESH)
        return carry


    near = rows <= 4 and cols <= 4
    up, down = my_row > 0, my_row < rows - 1
    left, right = my_col > 0, my_col < cols - 1
    if near:
        for there, axis, at in ((up, "row", my_row - 1), (down, "row", my_row + 1), (left, "col", my_col - 1), (right, "col", my_col + 1)):
            @pl.when(there)
            def _(axis=axis, at=at):
                pl.semaphore_signal(barrier, inc=1, device_id={axis: at}, device_id_type=MESH)
    else:
        lax.fori_loop(1, count, greet, 0)

    row_at = lax.broadcasted_iota(jnp.int32, (high, wide), 0)
    lane = lax.broadcasted_iota(jnp.int32, (high, wide), 1)
    pair = jnp.where(lane == wide - 1, 0, (lane + 1) // 2)
    edge = jnp.where(lane == 0, -1.0, jnp.where(lane == wide - 1, 1.0, 0.0))

    for there, ref in ((up, got_lo), (down, got_hi), (left, got_l), (right, got_r), (up, pgot_lo), (down, pgot_hi),
                       (left, pgot_l), (right, pgot_r)):
        @pl.when(jnp.logical_not(there))
        def _(ref=ref):
            ref[...] = jnp.zeros_like(ref)

    corners = []
    for q, (dr, dc) in enumerate(((1, 1), (1, -1), (-1, 1), (-1, -1))):
        sends = jnp.logical_and(down if dr > 0 else up, right if dc > 0 else left)
        gets = jnp.logical_and(up if dr > 0 else down, left if dc > 0 else right)
        corners.append((q, dr, dc, sends, gets))

        @pl.when(jnp.logical_not(gets))
        def _(q=q):
            for p in range(1, KRYLOV, 2):
                got_c[p, q] = jnp.zeros((1, wide), jnp.float32)

    def diagonals(p):
        made = []
        for q, dr, dc, sends, gets in corners:
            at = high - 1 if dr > 0 else 0
            made.append((sends, gets, pltpu.make_async_remote_copy(
                src_ref=put_t.at[p, at:at + 1], dst_ref=got_c.at[p, q],
                send_sem=csend.at[p, q], recv_sem=crecv.at[p, q],
                device_id={"row": lax.rem(my_row + dr + rows, rows), "col": lax.rem(my_col + dc + cols, cols)},
                device_id_type=MESH)))
        return made

    def blocks():
        def make(src, dst, axis, mine, step, size, q):
            return pltpu.make_async_remote_copy(
                src_ref=src, dst_ref=dst, send_sem=psend.at[q], recv_sem=precv.at[q],
                device_id={axis: lax.rem(mine + step + size, size)}, device_id_type=MESH)
        return [
            (up, down, make(pput_lo, pgot_hi, "row", my_row, -1, rows, 0)),
            (down, up, make(pput_hi, pgot_lo, "row", my_row, 1, rows, 1)),
            (left, right, make(pput_t, pgot_r, "col", my_col, -1, cols, 2)),
            (right, left, make(pput_t, pgot_l, "col", my_col, 1, cols, 3)),
        ]

    def transfers(p, lo=None, hi=None):
        def make(src, dst, axis, mine, step, size, q):
            return pltpu.make_async_remote_copy(
                src_ref=src, dst_ref=dst.at[p], send_sem=ssem.at[p, q], recv_sem=rsem.at[p, q],
                device_id={axis: lax.rem(mine + step + size, size)}, device_id_type=MESH)
        return [
            (up, down, make(put_lo.at[p] if lo is None else lo, got_hi, "row", my_row, -1, rows, 0)),
            (down, up, make(put_hi.at[p] if hi is None else hi, got_lo, "row", my_row, 1, rows, 1)),
            (left, right, make(put_t.at[p], got_r, "col", my_col, -1, cols, 2)),
            (right, left, make(put_t.at[p], got_l, "col", my_col, 1, cols, 3)),
        ]

    def tile_of(v):
        tile = jnp.zeros((high, wide), jnp.float32)
        for s in range(species):
            moved = pltpu.roll(v[s], 2 * s, 1) if s else v[s]
            tile = jnp.where(pair == s, moved, tile)
        return tile

    def pack(p, v):
        for s in range(species):
            put_lo[p, s:s + 1, :] = v[s, 0:1, :]
            put_hi[p, s:s + 1, :] = v[s, high - 1:high, :]
        put_t[p] = tile_of(v)

    def pack_blocks():
        def one(t, carry):
            block = prec[:, t]
            for s in range(species):
                pput_lo[t, s:s + 1, :] = block[s, 0:1, :]
                pput_hi[t, s:s + 1, :] = block[s, high - 1:high, :]
            pput_t[t] = tile_of(block)
            return carry
        lax.fori_loop(0, species, one, 0)

    def send(made):
        for sends, _, copy in made:
            @pl.when(sends)
            def _(copy=copy):
                copy.start()

    def receive(made):
        for _, gets, copy in made:
            @pl.when(gets)
            def _(copy=copy):
                copy.wait_recv()

    def sent(made):
        for sends, _, copy in made:
            @pl.when(sends)
            def _(copy=copy):
                copy.wait_send()

    def own_part(k):
        low = top = jnp.zeros((species, wide), jnp.float32)
        west = east = jnp.zeros((high, wide), jnp.float32)
        for t in range(species):
            d = ds[k, t]
            ax, ay = cx[t], cy[t]
            low = low + pgot_lo[t] * (ax[0:1] * d[0:1])
            top = top - pgot_hi[t] * (ax[0:1] * d[high - 1:high])
            west = west + pgot_l[t] * (ay * d[:, 0:1])
            east = east - pgot_r[t] * (ay * d[:, wide - 1:wide])
        return low, top, west, east

    def complete(p, own):
        low, top, west, east = own
        first = lax.broadcasted_iota(jnp.int32, (1, wide), 1) == 0
        near_row, far_row = row_at == 0, row_at == high - 1
        lines = [got_c[p, q] for q in range(4)]
        for t in range(species):
            odd, even = (2 * t - 1) % wide, 2 * t
            ul, dl = lines[0][:, odd:odd + 1], lines[2][:, odd:odd + 1]
            ur, dr = lines[1][:, even:even + 1], lines[3][:, even:even + 1]
            ax, ends = cx[t], cs[t, 0:1, :]
            low = low + pgot_lo[t] * (ends * jnp.where(first, ul, ur))
            top = top + pgot_hi[t] * (ends * jnp.where(first, dl, dr))
            west = west + pgot_l[t] * (ax * jnp.where(near_row, -ul, jnp.where(far_row, dl, 0.0)))
            east = east + pgot_r[t] * (ax * jnp.where(near_row, -ur, jnp.where(far_row, dr, 0.0)))
        got_lo[p + 1] += low
        got_hi[p + 1] += top
        got_l[p + 1] += west
        got_r[p + 1] += east

    def inner(v):
        parts = []
        for s in range(species):
            f = v[s]
            dx = jnp.where(row_at == high - 1, 0.0, pltpu.roll(f, high - 1, 0)) - jnp.where(
                row_at == 0, 0.0, pltpu.roll(f, 1, 0))
            dy = jnp.where(lane == wide - 1, 0.0, pltpu.roll(f, wide - 1, 1)) - jnp.where(
                lane == 0, 0.0, pltpu.roll(f, 1, 1))
            parts.append(cx[s] * dx + cy[s] * dy)
        return jnp.stack(parts)

    def outer(p):
        both = jnp.where(lax.rem(lane, 2) == 1, pltpu.roll(got_l[p], 2, 1), got_r[p])
        parts = []
        for s in range(species):
            moved = pltpu.roll(both, wide - 2 * s - 1, 1)
            ends = jnp.where(row_at == high - 1, got_hi[p, s:s + 1, :], 0.0) - jnp.where(
                row_at == 0, got_lo[p, s:s + 1, :], 0.0)
            parts.append(cx[s] * ends + cs[s] * moved)
        return jnp.stack(parts)

    def blockmul(matrix, field):
        total = matrix[:, 0] * field(0)[None]
        for t in range(1, species):
            total = total + matrix[:, t] * field(t)[None]
        return total

    def dots(k, upto):
        line = grow[...]
        at = lax.broadcasted_iota(jnp.int32, line.shape, 1)
        mine = vs[k]
        for j in range(upto):
            by_cell = jnp.sum(mine * vs[j], axis=0)
            value = jnp.sum(jnp.sum(by_cell, axis=0, keepdims=True), axis=1, keepdims=True)
            line = jnp.where(at == k * (KRYLOV + 1) + j, value, line)
        grow[...] = line

    if near:
        beside = sum(there.astype(jnp.int32) for there in (up, down, left, right))
        pl.semaphore_wait(barrier, beside)
    else:
        pl.semaphore_wait(barrier, count - 1)
    state_out = transfers(0, state_h.at[:, 0, :], state_h.at[:, high - 1, :])
    send(state_out[:2])
    copies[0].wait()
    put_t[0] = tile_of(y[...])
    send(state_out[2:])
    copies[1].wait()
    for s in range(species):
        cx[s] = jnp.full((high, wide), 0.5 * GAMMA * vel[0, s])
        cy[s] = jnp.full((high, wide), 0.5 * GAMMA * vel[1, s])
        cs[s] = cy[s] * edge
    for k in range(1, KRYLOV):
        vs[k] = jnp.zeros_like(y)
    grow[...] = jnp.zeros_like(grow)
    for copy in copies[2:5]:
        copy.wait()
    now = y[...]
    copies[5].wait()
    pack_blocks()
    send(blocks())
    loss = quad[...] * now
    diag[...] = 1.0 + (2.0 * GAMMA) * loss
    start = hist[...] - now - GAMMA * (loss * now) + GAMMA * blockmul(rates, lambda t: y[t]) - inner(now)
    receive(state_out)
    vs[0] = start - outer(0)

    def apply(k):
        return diag[...] * ds[k] - SHIFT * vs[k] - GAMMA * blockmul(rates, lambda t: ds[k, t]) + inner(ds[k])

    def two_steps(j, carry):
        k, p = 2 * j, 2 * j + 1
        ds[k] = blockmul(prec, lambda t: vs[k, t])
        pack(p, ds[k])
        send(transfers(p))
        send(diagonals(p))
        vs[k + 1] = apply(k)
        pack(p + 1, blockmul(prec, lambda t: vs[k + 1, t]))
        send(transfers(p + 1))
        dots(k, KRYLOV)

        @pl.when(j == 0)
        def _():
            receive(blocks())

        own = own_part(k)
        receive(transfers(p))
        vs[k + 1] = vs[k + 1] + outer(p)
        ds[k + 1] = blockmul(prec, lambda t: vs[k + 1, t])
        vs[k + 2] = apply(k + 1)
        dots(k + 1, KRYLOV)
        receive(transfers(p + 1))
        receive(diagonals(p))
        complete(p, own)
        vs[k + 2] = vs[k + 2] + outer(p + 1)
        return carry

    lax.fori_loop(0, KRYLOV // 2, two_steps, 0)
    dots(KRYLOV, KRYLOV + 1)
    slots[me] = grow[...]

    def share(o):
        index, where = other(o)
        put = pltpu.make_async_remote_copy(
            src_ref=grow, dst_ref=slots.at[me], send_sem=gsend.at[o], recv_sem=grecv.at[me],
            device_id=where, device_id_type=MESH)
        take = pltpu.make_async_remote_copy(
            src_ref=grow, dst_ref=slots.at[index], send_sem=gsend.at[o], recv_sem=grecv.at[index],
            device_id=where, device_id_type=MESH)
        return put, take

    def put_all(o, carry):
        share(o)[0].start()
        return carry

    def take_all(o, carry):
        share(o)[1].wait_recv()
        return carry

    def put_done(o, carry):
        share(o)[0].wait_send()
        return carry

    lax.fori_loop(1, count, put_all, 0)
    sent(state_out)
    for p in range(1, KRYLOV + 1):
        sent(transfers(p))
    for p in range(1, KRYLOV, 2):
        sent(diagonals(p))
    sent(blocks())
    lax.fori_loop(1, count, take_all, 0)
    total = jnp.sum(slots[...], axis=0)
    at = lax.broadcasted_iota(jnp.int32, total.shape, 1)
    gram = [[jnp.sum(jnp.where(at == k * (KRYLOV + 1) + j, total, 0.0), axis=1, keepdims=True)
             for j in range(k + 1)] for k in range(KRYLOV + 1)]
    coef, residual = small_solve(gram)
    lin[0] = residual[0, 0]
    result = y[...]
    for k in range(KRYLOV):
        result = result + jnp.broadcast_to(coef[k], (high, wide))[None] * ds[k]
    out[...] = result
    lax.fori_loop(1, count, put_done, 0)


def body(rows, cols, state, history, rates, quadratic, velocity, precond):
    species, high, wide = state.shape
    field = (species, high, wide)
    phases = KRYLOV + 1
    vmem = lambda *shape: pltpu.VMEM(shape, jnp.float32)
    anywhere = pl.BlockSpec(memory_space=pl.ANY)
    updated, residual = pl.pallas_call(
        functools.partial(kernel, rows, cols),
        out_shape=(pltpu.VMEM(field, jnp.float32), jax.ShapeDtypeStruct((1,), jnp.float32)),
        in_specs=[anywhere] * 6,
        out_specs=(pl.BlockSpec(memory_space=pltpu.VMEM), pl.BlockSpec(memory_space=pltpu.SMEM)),
        scratch_shapes=[
            pltpu.SMEM(velocity.shape[::-1], jnp.float32),
            vmem(*field), vmem(*field), vmem(species, *field), vmem(*field), vmem(species, *field),
            pltpu.SemaphoreType.DMA((6,)),
            vmem(phases, *field), vmem(KRYLOV, *field),
            vmem(*field), vmem(*field), vmem(*field), vmem(*field),
            vmem(phases, species, wide), vmem(phases, species, wide), vmem(phases, high, wide),
            vmem(phases, species, wide), vmem(phases, species, wide),
            vmem(phases, high, wide), vmem(phases, high, wide),
            pltpu.SemaphoreType.DMA((phases, 4)), pltpu.SemaphoreType.DMA((phases, 4)),
            vmem(1, wide), vmem(rows * cols, 1, wide),
            pltpu.SemaphoreType.DMA((rows * cols,)), pltpu.SemaphoreType.DMA((rows * cols,)),
            vmem(species, species, wide), vmem(species, species, wide), vmem(species, high, wide),
            vmem(species, species, wide), vmem(species, species, wide),
            vmem(species, high, wide), vmem(species, high, wide),
            pltpu.SemaphoreType.DMA((4,)), pltpu.SemaphoreType.DMA((4,)),
            vmem(phases, 4, 1, wide),
            pltpu.SemaphoreType.DMA((phases, 4)), pltpu.SemaphoreType.DMA((phases, 4)),
        ],
        compiler_params=pltpu.CompilerParams(collective_id=0, has_side_effects=True),
    )(state, history, rates, quadratic, velocity.T, precond)
    return updated, residual


def solution(mesh):
    cells = P(None, ("parts", "row"), "col")
    blocks = P(None, None, ("parts", "row"), "col")
    return jax.shard_map(
        functools.partial(body, mesh.shape["row"], mesh.shape["col"]),
        mesh=mesh,
        in_specs=(cells, cells, blocks, cells, P(), blocks),
        out_specs=(cells, P("parts")),
        check_vma=False,
    )
```

```python
import functools

import jax
import jax.numpy as jnp
from jax import lax
from jax.experimental import pallas as pl
from jax.experimental.pallas import tpu as pltpu
from jax.sharding import PartitionSpec as P

KRYLOV = 4
GAMMA = 0.4
EPS = 1e-12
SHIFT = 1.5
MESH = pl.DeviceIdType.MESH


def small_solve(gram):
    width = KRYLOV
    norm2 = gram[0][0] + EPS
    beta = jnp.sqrt(norm2)
    scale = 1.0 / norm2
    g = {(i, j): gram[j][i] * scale for j in range(width + 1) for i in range(j + 1)}
    one = jnp.ones_like(beta)
    tri = {(0, 0): one}
    inv = [one]
    sub = []
    for j in range(width + 1):
        for i in range(min(j, width)):
            value = g[i, j]
            for m in range(i):
                value = value - tri[m, i] * tri[m, j]
            tri[i, j] = value * inv[i]
        if j:
            left = g[j, j]
            for m in range(j):
                left = left - tri[m, j] * tri[m, j]
            size = jnp.sqrt(jnp.maximum(left, 0.0) * inv[j - 1] * inv[j - 1] + EPS)
            sub.append(size)
            tri[j, j] = tri[j - 1, j - 1] * size
            inv.append(1.0 / tri[j, j])
    hess = {}
    for k in range(width):
        for i in range(k + 1):
            value = tri[i, k + 1] + SHIFT * tri[i, k]
            for m in range(max(i - 1, 0), k):
                value = value - hess[i, m] * tri[m, k]
            hess[i, k] = value * inv[k]
        hess[k + 1, k] = sub[k]
    rot = [beta]
    for k in range(width):
        first, second = hess[k, k], hess[k + 1, k]
        inverse = 1.0 / jnp.sqrt(first * first + second * second)
        cosine, sine = first * inverse, second * inverse
        for j in range(k, width):
            top = hess[k, j]
            low = hess.get((k + 1, j))
            hess[k, j] = cosine * top + sine * low
            hess[k + 1, j] = cosine * low - sine * top
        rot.append(-sine * rot[k])
        rot[k] = cosine * rot[k]
    coef = [None] * width
    for k in reversed(range(width)):
        value = rot[k]
        for m in range(k + 1, width):
            value = value - hess[k, m] * coef[m]
        coef[k] = value / hess[k, k]
    out = [None] * width
    for k in reversed(range(width)):
        value = coef[k]
        for m in range(k + 1, width):
            value = value - tri[k, m] * out[m]
        out[k] = value * inv[k]
    return [c / beta for c in out], jnp.abs(rot[width])


def kernel(rows, cols, state_h, hist_h, rates_h, quad_h, vel_h, prec_h, out, lin,
           vel, y, hist, rates, quad, prec, loads, vs, ds, diag, cx, cy, cs,
           put_lo, put_hi, put_t, got_lo, got_hi, got_l, got_r, ssem, rsem,
           grow, slots, gsend, grecv,
           pput_lo, pput_hi, pput_t, pgot_lo, pgot_hi, pgot_l, pgot_r, psend, precv, got_c, csend, crecv):
    species, high, wide = y.shape
    my_row, my_col = lax.axis_index("row"), lax.axis_index("col")
    count = rows * cols
    me = my_row * cols + my_col
    pairs = [(state_h, y), (vel_h, vel), (rates_h, rates), (quad_h, quad), (hist_h, hist), (prec_h, prec)]
    copies = [pltpu.make_async_copy(a, b, loads.at[i]) for i, (a, b) in enumerate(pairs)]
    for copy in copies:
        copy.start()

    barrier = pltpu.get_barrier_semaphore()

    def other(o):
        index = lax.rem(me + o, count)
        return index, {"row": index // cols, "col": lax.rem(index, cols)}

    def greet(o, carry):
        pl.semaphore_signal(barrier, inc=1, device_id=other(o)[1], device_id_type=MESH)
        return carry


    near = rows <= 4 and cols <= 4
    up, down = my_row > 0, my_row < rows - 1
    left, right = my_col > 0, my_col < cols - 1
    if near:
        for there, axis, at in ((up, "row", my_row - 1), (down, "row", my_row + 1), (left, "col", my_col - 1), (right, "col", my_col + 1)):
            @pl.when(there)
            def _(axis=axis, at=at):
                pl.semaphore_signal(barrier, inc=1, device_id={axis: at}, device_id_type=MESH)
    else:
        lax.fori_loop(1, count, greet, 0)

    row_at = lax.broadcasted_iota(jnp.int32, (high, wide), 0)
    lane = lax.broadcasted_iota(jnp.int32, (high, wide), 1)
    pair = jnp.where(lane == wide - 1, 0, (lane + 1) // 2)
    edge = jnp.where(lane == 0, -1.0, jnp.where(lane == wide - 1, 1.0, 0.0))

    for there, ref in ((up, got_lo), (down, got_hi), (left, got_l), (right, got_r), (up, pgot_lo), (down, pgot_hi),
                       (left, pgot_l), (right, pgot_r)):
        @pl.when(jnp.logical_not(there))
        def _(ref=ref):
            ref[...] = jnp.zeros_like(ref)

    corners = []
    for q, (dr, dc) in enumerate(((1, 1), (1, -1), (-1, 1), (-1, -1))):
        sends = jnp.logical_and(down if dr > 0 else up, right if dc > 0 else left)
        gets = jnp.logical_and(up if dr > 0 else down, left if dc > 0 else right)
        corners.append((q, dr, dc, sends, gets))

        @pl.when(jnp.logical_not(gets))
        def _(q=q):
            for p in range(1, KRYLOV, 2):
                got_c[p, q] = jnp.zeros((1, wide), jnp.float32)

    def diagonals(p):
        made = []
        for q, dr, dc, sends, gets in corners:
            at = high - 1 if dr > 0 else 0
            made.append((sends, gets, pltpu.make_async_remote_copy(
                src_ref=put_t.at[p, at:at + 1], dst_ref=got_c.at[p, q],
                send_sem=csend.at[p, q], recv_sem=crecv.at[p, q],
                device_id={"row": lax.rem(my_row + dr + rows, rows), "col": lax.rem(my_col + dc + cols, cols)},
                device_id_type=MESH)))
        return made

    def blocks():
        def make(src, dst, axis, mine, step, size, q):
            return pltpu.make_async_remote_copy(
                src_ref=src, dst_ref=dst, send_sem=psend.at[q], recv_sem=precv.at[q],
                device_id={axis: lax.rem(mine + step + size, size)}, device_id_type=MESH)
        return [
            (up, down, make(pput_lo, pgot_hi, "row", my_row, -1, rows, 0)),
            (down, up, make(pput_hi, pgot_lo, "row", my_row, 1, rows, 1)),
            (left, right, make(pput_t, pgot_r, "col", my_col, -1, cols, 2)),
            (right, left, make(pput_t, pgot_l, "col", my_col, 1, cols, 3)),
        ]

    def transfers(p):
        def make(src, dst, axis, mine, step, size, q):
            return pltpu.make_async_remote_copy(
                src_ref=src, dst_ref=dst.at[p], send_sem=ssem.at[p, q], recv_sem=rsem.at[p, q],
                device_id={axis: lax.rem(mine + step + size, size)}, device_id_type=MESH)
        return [
            (up, down, make(put_lo.at[p], got_hi, "row", my_row, -1, rows, 0)),
            (down, up, make(put_hi.at[p], got_lo, "row", my_row, 1, rows, 1)),
            (left, right, make(put_t.at[p], got_r, "col", my_col, -1, cols, 2)),
            (right, left, make(put_t.at[p], got_l, "col", my_col, 1, cols, 3)),
        ]

    def tile_of(v):
        tile = jnp.zeros((high, wide), jnp.float32)
        for s in range(species):
            moved = pltpu.roll(v[s], 2 * s, 1) if s else v[s]
            tile = jnp.where(pair == s, moved, tile)
        return tile

    def pack(p, v):
        for s in range(species):
            put_lo[p, s:s + 1, :] = v[s, 0:1, :]
            put_hi[p, s:s + 1, :] = v[s, high - 1:high, :]
        put_t[p] = tile_of(v)

    def pack_blocks():
        def one(t, carry):
            block = prec[:, t]
            for s in range(species):
                pput_lo[t, s:s + 1, :] = block[s, 0:1, :]
                pput_hi[t, s:s + 1, :] = block[s, high - 1:high, :]
            pput_t[t] = tile_of(block)
            return carry
        lax.fori_loop(0, species, one, 0)

    def send(made):
        for sends, _, copy in made:
            @pl.when(sends)
            def _(copy=copy):
                copy.start()

    def receive(made):
        for _, gets, copy in made:
            @pl.when(gets)
            def _(copy=copy):
                copy.wait_recv()

    def sent(made):
        for sends, _, copy in made:
            @pl.when(sends)
            def _(copy=copy):
                copy.wait_send()

    def own_part(k):
        low = top = jnp.zeros((species, wide), jnp.float32)
        west = east = jnp.zeros((high, wide), jnp.float32)
        for t in range(species):
            d = ds[k, t]
            ax, ay = cx[t], cy[t]
            low = low + pgot_lo[t] * (ax[0:1] * d[0:1])
            top = top - pgot_hi[t] * (ax[0:1] * d[high - 1:high])
            west = west + pgot_l[t] * (ay * d[:, 0:1])
            east = east - pgot_r[t] * (ay * d[:, wide - 1:wide])
        return low, top, west, east

    def complete(p, own):
        low, top, west, east = own
        first = lax.broadcasted_iota(jnp.int32, (1, wide), 1) == 0
        near_row, far_row = row_at == 0, row_at == high - 1
        lines = [got_c[p, q] for q in range(4)]
        for t in range(species):
            odd, even = (2 * t - 1) % wide, 2 * t
            ul, dl = lines[0][:, odd:odd + 1], lines[2][:, odd:odd + 1]
            ur, dr = lines[1][:, even:even + 1], lines[3][:, even:even + 1]
            ax, ends = cx[t], cs[t, 0:1, :]
            low = low + pgot_lo[t] * (ends * jnp.where(first, ul, ur))
            top = top + pgot_hi[t] * (ends * jnp.where(first, dl, dr))
            west = west + pgot_l[t] * (ax * jnp.where(near_row, -ul, jnp.where(far_row, dl, 0.0)))
            east = east + pgot_r[t] * (ax * jnp.where(near_row, -ur, jnp.where(far_row, dr, 0.0)))
        got_lo[p + 1] += low
        got_hi[p + 1] += top
        got_l[p + 1] += west
        got_r[p + 1] += east

    def inner(v):
        parts = []
        for s in range(species):
            f = v[s]
            dx = jnp.where(row_at == high - 1, 0.0, pltpu.roll(f, high - 1, 0)) - jnp.where(
                row_at == 0, 0.0, pltpu.roll(f, 1, 0))
            dy = jnp.where(lane == wide - 1, 0.0, pltpu.roll(f, wide - 1, 1)) - jnp.where(
                lane == 0, 0.0, pltpu.roll(f, 1, 1))
            parts.append(cx[s] * dx + cy[s] * dy)
        return jnp.stack(parts)

    def outer(p):
        both = jnp.where(lax.rem(lane, 2) == 1, pltpu.roll(got_l[p], 2, 1), got_r[p])
        parts = []
        for s in range(species):
            moved = pltpu.roll(both, wide - 2 * s - 1, 1)
            ends = jnp.where(row_at == high - 1, got_hi[p, s:s + 1, :], 0.0) - jnp.where(
                row_at == 0, got_lo[p, s:s + 1, :], 0.0)
            parts.append(cx[s] * ends + cs[s] * moved)
        return jnp.stack(parts)

    def blockmul(matrix, field):
        total = matrix[:, 0] * field(0)[None]
        for t in range(1, species):
            total = total + matrix[:, t] * field(t)[None]
        return total

    def dots(k, upto):
        line = grow[...]
        at = lax.broadcasted_iota(jnp.int32, line.shape, 1)
        mine = vs[k]
        for j in range(upto):
            by_cell = jnp.sum(mine * vs[j], axis=0)
            value = jnp.sum(jnp.sum(by_cell, axis=0, keepdims=True), axis=1, keepdims=True)
            line = jnp.where(at == k * (KRYLOV + 1) + j, value, line)
        grow[...] = line

    copies[0].wait()
    pack(0, y[...])
    if near:
        beside = sum(there.astype(jnp.int32) for there in (up, down, left, right))
        pl.semaphore_wait(barrier, beside)
    else:
        pl.semaphore_wait(barrier, count - 1)
    state_out = transfers(0)
    send(state_out)
    copies[1].wait()
    for s in range(species):
        cx[s] = jnp.full((high, wide), 0.5 * GAMMA * vel[0, s])
        cy[s] = jnp.full((high, wide), 0.5 * GAMMA * vel[1, s])
        cs[s] = cy[s] * edge
    for k in range(1, KRYLOV):
        vs[k] = jnp.zeros_like(y)
    grow[...] = jnp.zeros_like(grow)
    for copy in copies[2:5]:
        copy.wait()
    now = y[...]
    copies[5].wait()
    pack_blocks()
    send(blocks())
    loss = quad[...] * now
    diag[...] = 1.0 + (2.0 * GAMMA) * loss
    start = hist[...] - now - GAMMA * (loss * now) + GAMMA * blockmul(rates, lambda t: y[t]) - inner(now)
    receive(state_out)
    vs[0] = start - outer(0)

    def apply(k):
        return diag[...] * ds[k] - SHIFT * vs[k] - GAMMA * blockmul(rates, lambda t: ds[k, t]) + inner(ds[k])

    def two_steps(j, carry):
        k, p = 2 * j, 2 * j + 1
        ds[k] = blockmul(prec, lambda t: vs[k, t])
        pack(p, ds[k])
        send(transfers(p))
        send(diagonals(p))
        vs[k + 1] = apply(k)
        pack(p + 1, blockmul(prec, lambda t: vs[k + 1, t]))
        send(transfers(p + 1))
        dots(k, KRYLOV)

        @pl.when(j == 0)
        def _():
            receive(blocks())

        own = own_part(k)
        receive(transfers(p))
        vs[k + 1] = vs[k + 1] + outer(p)
        ds[k + 1] = blockmul(prec, lambda t: vs[k + 1, t])
        vs[k + 2] = apply(k + 1)
        dots(k + 1, KRYLOV)
        receive(transfers(p + 1))
        receive(diagonals(p))
        complete(p, own)
        vs[k + 2] = vs[k + 2] + outer(p + 1)
        return carry

    lax.fori_loop(0, KRYLOV // 2, two_steps, 0)
    dots(KRYLOV, KRYLOV + 1)
    slots[me] = grow[...]

    def share(o):
        index, where = other(o)
        put = pltpu.make_async_remote_copy(
            src_ref=grow, dst_ref=slots.at[me], send_sem=gsend.at[o], recv_sem=grecv.at[me],
            device_id=where, device_id_type=MESH)
        take = pltpu.make_async_remote_copy(
            src_ref=grow, dst_ref=slots.at[index], send_sem=gsend.at[o], recv_sem=grecv.at[index],
            device_id=where, device_id_type=MESH)
        return put, take

    def put_all(o, carry):
        share(o)[0].start()
        return carry

    def take_all(o, carry):
        share(o)[1].wait_recv()
        return carry

    def put_done(o, carry):
        share(o)[0].wait_send()
        return carry

    lax.fori_loop(1, count, put_all, 0)
    sent(state_out)
    for p in range(1, KRYLOV + 1):
        sent(transfers(p))
    for p in range(1, KRYLOV, 2):
        sent(diagonals(p))
    sent(blocks())
    lax.fori_loop(1, count, take_all, 0)
    total = jnp.sum(slots[...], axis=0)
    at = lax.broadcasted_iota(jnp.int32, total.shape, 1)
    gram = [[jnp.sum(jnp.where(at == k * (KRYLOV + 1) + j, total, 0.0), axis=1, keepdims=True)
             for j in range(k + 1)] for k in range(KRYLOV + 1)]
    coef, residual = small_solve(gram)
    lin[0] = residual[0, 0]
    result = y[...]
    for k in range(KRYLOV):
        result = result + jnp.broadcast_to(coef[k], (high, wide))[None] * ds[k]
    out[...] = result
    lax.fori_loop(1, count, put_done, 0)


def body(rows, cols, state, history, rates, quadratic, velocity, precond):
    species, high, wide = state.shape
    field = (species, high, wide)
    phases = KRYLOV + 1
    vmem = lambda *shape: pltpu.VMEM(shape, jnp.float32)
    anywhere = pl.BlockSpec(memory_space=pl.ANY)
    updated, residual = pl.pallas_call(
        functools.partial(kernel, rows, cols),
        out_shape=(pltpu.VMEM(field, jnp.float32), jax.ShapeDtypeStruct((1,), jnp.float32)),
        in_specs=[anywhere] * 6,
        out_specs=(pl.BlockSpec(memory_space=pltpu.VMEM), pl.BlockSpec(memory_space=pltpu.SMEM)),
        scratch_shapes=[
            pltpu.SMEM(velocity.shape[::-1], jnp.float32),
            vmem(*field), vmem(*field), vmem(species, *field), vmem(*field), vmem(species, *field),
            pltpu.SemaphoreType.DMA((6,)),
            vmem(phases, *field), vmem(KRYLOV, *field),
            vmem(*field), vmem(*field), vmem(*field), vmem(*field),
            vmem(phases, species, wide), vmem(phases, species, wide), vmem(phases, high, wide),
            vmem(phases, species, wide), vmem(phases, species, wide),
            vmem(phases, high, wide), vmem(phases, high, wide),
            pltpu.SemaphoreType.DMA((phases, 4)), pltpu.SemaphoreType.DMA((phases, 4)),
            vmem(1, wide), vmem(rows * cols, 1, wide),
            pltpu.SemaphoreType.DMA((rows * cols,)), pltpu.SemaphoreType.DMA((rows * cols,)),
            vmem(species, species, wide), vmem(species, species, wide), vmem(species, high, wide),
            vmem(species, species, wide), vmem(species, species, wide),
            vmem(species, high, wide), vmem(species, high, wide),
            pltpu.SemaphoreType.DMA((4,)), pltpu.SemaphoreType.DMA((4,)),
            vmem(phases, 4, 1, wide),
            pltpu.SemaphoreType.DMA((phases, 4)), pltpu.SemaphoreType.DMA((phases, 4)),
        ],
        compiler_params=pltpu.CompilerParams(collective_id=0, has_side_effects=True),
    )(state, history, rates, quadratic, velocity.T, precond)
    return updated, residual


def solution(mesh):
    cells = P(None, ("parts", "row"), "col")
    blocks = P(None, None, ("parts", "row"), "col")
    return jax.shard_map(
        functools.partial(body, mesh.shape["row"], mesh.shape["col"]),
        mesh=mesh,
        in_specs=(cells, cells, blocks, cells, P(), blocks),
        out_specs=(cells, P("parts")),
        check_vma=False,
    )
```
